32 devices in a mesh: row: 4 (over z), col: 8 (over y, x, core).
Axes of the slice: x: 2, y: 2, z: 4, core: 2. Of those that a mesh axis runs over, the one named last changes fastest.
Arguments:
- unfolding: bfloat16 [3072, 4096], P('row', 'col'), may hold values from -400 to 400
Outputs:
- regrouped: bfloat16 [256, 16, 3072], P('col', None, 'row')
The draws below stay inside these ranges and needn't reach their ends.
All inputs are finite; a program needn't handle non-finite values.
Results may differ from the reference program's by a relative error of at most 0.0062.
Values may be sent and summed in bfloat16 or wider, within the bound.
A program may use at most 64 MiB of HBM per device.

```python
import math
import jax
import jax.numpy as jnp

VIEWS = 16
PIXELS = 256
ITERS = 2
ROWS_DEV = 768
COLS = 4096
ROWS = 3072


def draw_unfolding(key, part):
    keys = jax.random.split(jax.random.fold_in(key, 11), 7)
    block_count = ROWS // ROWS_DEV
    block_order = jax.random.permutation(keys[3], block_count).astype(jnp.float32) / max(block_count - 1, 1)
    view_order = jax.random.permutation(keys[4], VIEWS).astype(jnp.float32) / max(VIEWS - 1, 1)
    row_block = block_order[jnp.arange(ROWS) // ROWS_DEV]
    col_block = view_order[jnp.arange(COLS) // PIXELS]
    row_scale = 3.0 ** row_block * jnp.exp(jax.random.uniform(keys[1], (ROWS,), jnp.float32) * math.log(10.0 / 3.0))
    spike_rank = 16
    shrink = min(1.0, ROWS / COLS)
    targets = [shrink * (0.4 + 1.0 * step / (spike_rank - 1)) for step in range(spike_rank)]
    denominator = COLS - 9.0 * sum(targets)
    left_vectors = jax.random.normal(keys[5], (ROWS, spike_rank), jnp.float32)
    right_vectors = jax.random.normal(keys[6], (COLS, spike_rank), jnp.float32)
    spikes = jnp.zeros((ROWS, COLS), jnp.float32)
    for step in range(spike_rank):
        amplitude = math.sqrt(9.0 * targets[step] / denominator)
        spikes = spikes + (amplitude * left_vectors[:, step])[:, None] * right_vectors[:, step][None, :]
    base = jax.random.normal(keys[0], (ROWS, COLS), jnp.float32)
    col_scale = 3.0 ** col_block * jnp.exp(jax.random.uniform(keys[2], (COLS,), jnp.float32) * math.log(10.0 / 3.0))
    inner = jnp.clip(base + spikes, -4.0, 4.0)
    return (inner * row_scale[:, None] * col_scale[None, :]).astype(jnp.bfloat16)


def setup_inputs(seed: int = 0) -> dict:
    key_list = jax.random.split(jax.random.key(seed), 2)
    return {
        "unfolding": draw_unfolding(jax.random.fold_in(key_list[1], 71), 0),
    }


def reference(unfolding):
    values = unfolding.astype(jnp.float32)
    sumsq = jnp.sum(values * values)
    current = (values * (math.sqrt(COLS) / (3.0 * jnp.sqrt(sumsq)))).astype(jnp.bfloat16)
    updated = current.astype(jnp.float32)
    for turn_index in range(ITERS):
        gram = jnp.dot(current.T, current, preferred_element_type=jnp.float32).astype(jnp.bfloat16)
        first = jnp.dot(current, gram, preferred_element_type=jnp.float32).astype(jnp.bfloat16)
        second = jnp.dot(first, gram, preferred_element_type=jnp.float32)
        updated = 1.875 * current.astype(jnp.float32) - 1.25 * first.astype(jnp.float32) + 0.375 * second
        if turn_index + 1 < ITERS:
            current = updated.astype(jnp.bfloat16)
    final = updated * math.sqrt(ROWS)
    cube = final.reshape(ROWS, VIEWS, PIXELS).transpose(2, 1, 0)
    return cube.astype(jnp.bfloat16)
```

```python
import functools
import math

import jax
import jax.numpy as jnp
from jax import lax
from jax.experimental import pallas as pl
from jax.experimental.pallas import tpu as pltpu
from jax.sharding import PartitionSpec as P

PIXELS = 256
ITERS = 2
COLS = 4096
MESH = pl.DeviceIdType.MESH


def exchange(nr, nc, x_ref, h_ref, xd_ref, ss_ref, xg, part, sendb, recvb, ssg,
             own_sem, a_s, a_r, b_s, b_r, d_s, d_r, s_s, s_r, f_s, f_r, g_s, g_r):
    r = lax.axis_index("row")
    c = lax.axis_index("col")
    rd = x_ref.shape[0]
    w = x_ref.shape[1] // nr
    st = part.shape[0]
    ch = st // nr
    direct = tuple(range(2, nc, 2))

    barrier = pltpu.get_barrier_semaphore()
    for k in range(1, nr):
        pl.semaphore_signal(barrier, inc=1, device_id=(lax.rem(r + k, nr), c), device_id_type=MESH)
    for d in (1,) + direct:
        pl.semaphore_signal(barrier, inc=1, device_id=(r, c ^ d), device_id_type=MESH)
    pl.semaphore_wait(barrier, nr - 1 + 1 + len(direct))

    def lanes(index):
        return pl.ds(pl.multiple_of(index * w, w), w)

    def rows(index, size):
        return pl.ds(pl.multiple_of(index * size, size), size)

    def to_row(src, dst, s_sem, r_sem, k):
        return pltpu.make_async_remote_copy(
            src_ref=src, dst_ref=dst, send_sem=s_sem, recv_sem=r_sem,
            device_id=(lax.rem(r + k, nr), c), device_id_type=MESH)

    def to_col(src, dst, s_sem, r_sem, d):
        return pltpu.make_async_remote_copy(
            src_ref=src, dst_ref=dst, send_sem=s_sem, recv_sem=r_sem,
            device_id=(r, c ^ d), device_id_type=MESH)

    def gather_col(view, s_sem, r_sem, ready):
        copies = {}

        def send(k, piece, slot, d):
            ref = view(k, piece)
            copies[k, slot] = to_col(ref, ref, s_sem.at[k, slot], r_sem.at[k, slot], d)
            copies[k, slot].start()

        for k in range(nr):
            ready(k)
            for d in direct + (1,):
                send(k, c, d, d)
        for k in range(nr):
            for d in direct:
                copies[k, d].wait_recv()
                send(k, c ^ d, d ^ 1, 1)
        for k in range(nr):
            for d in range(1, nc, 2):
                copies[k, d].wait_recv()
        for key in copies:
            copies[key].wait_send()

    a = {}
    for k in range(1, nr):
        a[k] = to_row(x_ref.at[:, lanes(lax.rem(r + k, nr))], xg.at[rows(r, rd), lanes(c)],
                      a_s.at[k], a_r.at[k], k)
        a[k].start()
    own = pltpu.make_async_copy(x_ref.at[:, lanes(r)], xg.at[rows(r, rd), lanes(c)], own_sem)
    own.start()

    def ready_x(k):
        if k == 0:
            own.wait()
        else:
            a[k].wait_recv()

    gather_col(lambda k, piece: xg.at[rows(lax.rem(r + nr - k, nr), rd), lanes(piece)],
               b_s, b_r, ready_x)
    for k in range(1, nr):
        a[k].wait_send()

    left = xg[rows(c, st), :]
    for j in range(nc // 2 + 1):
        right = xg[rows(lax.rem(c + j, nc), st), :]
        block = lax.dot_general(left, right, (((1,), (1,)), ((), ())), preferred_element_type=jnp.float32)
        part[:, j * st:(j + 1) * st] = block
        sendb[:, j * st:(j + 1) * st] = block.astype(jnp.bfloat16)

    dc = {}
    for k in range(1, nr):
        dc[k] = to_row(sendb.at[rows(lax.rem(r + k, nr), ch), :], recvb.at[k - 1], d_s.at[k], d_r.at[k], k)
        dc[k].start()

    step = 32

    def body(i, acc):
        v = xg[rows(i, step), :].astype(jnp.float32)
        v = v * v
        t = acc
        for m in range(step // 8):
            for n in range(v.shape[1] // 128):
                t = t + v[8 * m:8 * m + 8, 128 * n:128 * n + 128]
        return t

    ssg[0] = lax.fori_loop(0, xg.shape[0] // step, body, jnp.zeros((8, 128), jnp.float32))
    sc = {}
    for k in range(1, nr):
        sc[k] = to_row(ssg.at[0], ssg.at[k], s_s.at[k], s_r.at[k], k)
        sc[k].start()
    xd_ref[...] = xg[:, lanes(c)]

    for k in range(1, nr):
        dc[k].wait_recv()
    total = part[rows(r, ch), :]
    for k in range(1, nr):
        total = total + recvb[k - 1].astype(jnp.float32)
    h_ref[rows(c * nr + r, ch), :] = total.astype(jnp.bfloat16)

    fc = {}
    for k in range(1, nr):
        mine = h_ref.at[rows(c * nr + r, ch), :]
        fc[k] = to_row(mine, mine, f_s.at[k], f_r.at[k], k)
        fc[k].start()

    def ready_h(k):
        if k > 0:
            fc[k].wait_recv()

    gather_col(lambda k, piece: h_ref.at[rows(piece * nr + lax.rem(r + nr - k, nr), ch), :],
               g_s, g_r, ready_h)
    for k in range(1, nr):
        sc[k].wait_recv()
    tot = ssg[0]
    for k in range(1, nr):
        tot = tot + ssg[k]
    ss_ref[...] = tot
    for k in range(1, nr):
        dc[k].wait_send()
        sc[k].wait_send()
        fc[k].wait_send()


def row_gram(unfolding, nr, nc):
    rd, cd = unfolding.shape
    total_rows = rd * nr
    w = cd // nr
    st = total_rows // nc
    half = (nc // 2 + 1) * st
    vm = pl.BlockSpec(memory_space=pltpu.VMEM)
    dma = pltpu.SemaphoreType.DMA
    stripes, mine, squares = pl.pallas_call(
        functools.partial(exchange, nr, nc),
        out_shape=(
            jax.ShapeDtypeStruct((total_rows, half), jnp.bfloat16),
            jax.ShapeDtypeStruct((total_rows, w), jnp.bfloat16),
            jax.ShapeDtypeStruct((8, 128), jnp.float32),
        ),
        in_specs=[vm],
        out_specs=(vm, vm, vm),
        scratch_shapes=[
            pltpu.VMEM((total_rows, nc * w), jnp.bfloat16),
            pltpu.VMEM((st, half), jnp.float32),
            pltpu.VMEM((st, half), jnp.bfloat16),
            pltpu.VMEM((nr - 1, st // nr, half), jnp.bfloat16),
            pltpu.VMEM((nr, 8, 128), jnp.float32),
            dma, dma((nr,)), dma((nr,)), dma((nr, nc)), dma((nr, nc)),
            dma((nr,)), dma((nr,)), dma((nr,)), dma((nr,)),
            dma((nr,)), dma((nr,)), dma((nr, nc)), dma((nr, nc)),
        ],
        compiler_params=pltpu.CompilerParams(
            collective_id=0, has_side_effects=True, vmem_limit_bytes=56 * 1024 * 1024),
    )(unfolding)
    return stripes, mine, jnp.sum(squares)


def expand(stripes, nc):
    st = stripes.shape[0] // nc

    def block(i, j):
        d = (j - i) % nc
        if d <= nc // 2:
            return stripes[i * st:(i + 1) * st, d * st:(d + 1) * st]
        d = (i - j) % nc
        return stripes[j * st:(j + 1) * st, d * st:(d + 1) * st].T

    return jnp.concatenate(
        [jnp.concatenate([block(i, j) for j in range(nc)], axis=1) for i in range(nc)], axis=0)


def local_rows(unfolding, nr, nc):
    rd, cd = unfolding.shape
    stripes, mine, sumsq = row_gram(unfolding, nr, nc)
    gram = expand(stripes, nc)
    factor = math.sqrt(COLS) / (3.0 * jnp.sqrt(sumsq))
    square = factor * factor

    def times(v):
        return square * lax.dot_general(
            v.astype(jnp.bfloat16), gram, (((1,), (0,)), ((), ())), preferred_element_type=jnp.float32)

    def poly(v, op):
        one = op(v)
        return 1.875 * v - 1.25 * one + 0.375 * op(one)

    def apply_op(level):
        if level == 0:
            return times
        lower = apply_op(level - 1)
        return lambda v: lower(poly(poly(v, lower), lower))

    value = factor * mine.T.astype(jnp.float32)
    for turn_index in range(ITERS):
        value = poly(value, apply_op(turn_index))
    final = (value * math.sqrt(rd * nr)).astype(jnp.bfloat16)
    cols = lax.all_to_all(final, "row", split_axis=1, concat_axis=0, tiled=True)
    cube = cols.reshape(cd // PIXELS, PIXELS, rd).transpose(1, 0, 2)
    return lax.all_to_all(cube, "col", split_axis=0, concat_axis=1, tiled=True)


def local_cols(unfolding):
    rows_dev = unfolding.shape[0]
    cols_dev = unfolding.shape[1]
    total_rows = rows_dev * lax.axis_size("row")
    values = unfolding.astype(jnp.float32)
    sumsq = lax.psum(jnp.sum(values * values), ("row", "col"))
    factor = math.sqrt(COLS) / (3.0 * jnp.sqrt(sumsq))
    current = (values * factor).astype(jnp.bfloat16)
    updated = current.astype(jnp.float32)
    for turn_index in range(ITERS):
        gathered = lax.all_gather(current, "col", axis=1, tiled=True)
        partial_gram = lax.dot_general(
            current, gathered, (((0,), (0,)), ((), ())), preferred_element_type=jnp.float32
        )
        shares = lax.psum_scatter(partial_gram, "row", scatter_dimension=1, tiled=True).astype(
            jnp.bfloat16
        )
        gram_rows = lax.all_gather(shares, "row", axis=1, tiled=True)
        first = lax.dot_general(
            gathered, gram_rows, (((1,), (1,)), ((), ())), preferred_element_type=jnp.float32
        ).astype(jnp.bfloat16)
        second = lax.dot_general(
            lax.all_gather(first, "col", axis=1, tiled=True),
            gram_rows,
            (((1,), (1,)), ((), ())),
            preferred_element_type=jnp.float32,
        )
        updated = (
            1.875 * current.astype(jnp.float32) - 1.25 * first.astype(jnp.float32) + 0.375 * second
        )
        if turn_index + 1 < ITERS:
            current = updated.astype(jnp.bfloat16)
    final = updated * math.sqrt(total_rows)
    view_count = cols_dev // PIXELS
    cube = final.reshape(rows_dev, view_count, PIXELS).transpose(2, 1, 0).astype(jnp.bfloat16)
    return lax.all_to_all(cube, "col", split_axis=0, concat_axis=1, tiled=True)


def solution(mesh):
    nr, nc = mesh.shape["row"], mesh.shape["col"]

    def local(unfolding):
        rd, cd = unfolding.shape
        fits = cd % (128 * nr) == 0 and nc % 2 == 0 and (rd * nr) % (16 * nr * nc) == 0
        if rd * nr <= cd * nc and fits:
            return local_rows(unfolding, nr, nc)
        return local_cols(unfolding)

    return jax.shard_map(
        local,
        mesh=mesh,
        in_specs=(P("row", "col"),),
        out_specs=P("col", None, "row"),
        check_vma=False,
    )
```

```python
import functools
import math

import jax
import jax.numpy as jnp
from jax import lax
from jax.experimental import pallas as pl
from jax.experimental.pallas import tpu as pltpu
from jax.sharding import PartitionSpec as P

PIXELS = 256
ITERS = 2
COLS = 4096
MESH = pl.DeviceIdType.MESH


def exchange(nr, nc, x_ref, out_ref, h_ref, xg, part, sendb, recvb, ssg, full, floats, halves, turned,
             own_sem, a_s, a_r, b_s, b_r, d_s, d_r, s_s, s_r, f_s, f_r, g_s, g_r, o_s, o_r):
    r = lax.axis_index("row")
    c = lax.axis_index("col")
    rd = x_ref.shape[0]
    w = x_ref.shape[1] // nr
    st = part.shape[0]
    ch = st // nr
    direct = tuple(range(2, nc, 2))

    barrier = pltpu.get_barrier_semaphore()
    for k in range(nr):
        for m in range(nc):
            if k or m:
                pl.semaphore_signal(
                    barrier, inc=1, device_id=(lax.rem(r + k, nr), lax.rem(c + m, nc)), device_id_type=MESH)
    pl.semaphore_wait(barrier, nr * nc - 1)

    def lanes(index):
        return pl.ds(pl.multiple_of(index * w, w), w)

    def rows(index, size):
        return pl.ds(pl.multiple_of(index * size, size), size)

    def to_row(src, dst, s_sem, r_sem, k):
        return pltpu.make_async_remote_copy(
            src_ref=src, dst_ref=dst, send_sem=s_sem, recv_sem=r_sem,
            device_id=(lax.rem(r + k, nr), c), device_id_type=MESH)

    def to_col(src, dst, s_sem, r_sem, d):
        return pltpu.make_async_remote_copy(
            src_ref=src, dst_ref=dst, send_sem=s_sem, recv_sem=r_sem,
            device_id=(r, c ^ d), device_id_type=MESH)

    def gather_col(view, s_sem, r_sem, ready, landed):
        copies = {}

        def send(k, piece, slot, d):
            ref = view(k, piece)
            copies[k, slot] = to_col(ref, ref, s_sem.at[k, slot], r_sem.at[k, slot], d)
            copies[k, slot].start()

        for k in range(nr):
            ready(k)
            for d in direct + (1,):
                send(k, c, d, d)
        for k in range(nr):
            for d in direct:
                copies[k, d].wait_recv()
                send(k, c ^ d, d ^ 1, 1)
        for d in (0,) + direct + tuple(range(1, nc, 2)):
            if d % 2:
                for k in range(nr):
                    copies[k, d].wait_recv()
            landed(c ^ d)
        for key in copies:
            copies[key].wait_send()

    a = {}
    for k in range(1, nr):
        a[k] = to_row(x_ref.at[:, lanes(lax.rem(r + k, nr))], xg.at[rows(r, rd), lanes(c)],
                      a_s.at[k], a_r.at[k], k)
        a[k].start()
    own = pltpu.make_async_copy(x_ref.at[:, lanes(r)], xg.at[rows(r, rd), lanes(c)], own_sem)
    own.start()

    def ready_x(k):
        if k == 0:
            own.wait()
        else:
            a[k].wait_recv()

    gather_col(lambda k, piece: xg.at[rows(lax.rem(r + nr - k, nr), rd), lanes(piece)],
               b_s, b_r, ready_x, lambda piece: None)
    for k in range(1, nr):
        a[k].wait_send()

    left = xg[rows(c, st), :]
    for j in range(nc // 2 + 1):
        right = xg[rows(lax.rem(c + j, nc), st), :]
        block = lax.dot_general(left, right, (((1,), (1,)), ((), ())), preferred_element_type=jnp.float32)
        part[:, j * st:(j + 1) * st] = block
        sendb[:, j * st:(j + 1) * st] = block.astype(jnp.bfloat16)

    dc = {}
    for k in range(1, nr):
        dc[k] = to_row(sendb.at[rows(lax.rem(r + k, nr), ch), :], recvb.at[k - 1], d_s.at[k], d_r.at[k], k)
        dc[k].start()

    step = 32

    def body(i, acc):
        v = xg[rows(i, step), :].astype(jnp.float32)
        v = v * v
        t = acc
        for m in range(step // 8):
            for n in range(v.shape[1] // 128):
                t = t + v[8 * m:8 * m + 8, 128 * n:128 * n + 128]
        return t

    ssg[0] = lax.fori_loop(0, xg.shape[0] // step, body, jnp.zeros((8, 128), jnp.float32))
    sc = {}
    for k in range(1, nr):
        sc[k] = to_row(ssg.at[0], ssg.at[k], s_s.at[k], s_r.at[k], k)
        sc[k].start()
    for k in range(1, nr):
        dc[k].wait_recv()
    total = part[rows(r, ch), :]
    for k in range(1, nr):
        total = total + recvb[k - 1].astype(jnp.float32)
    h_ref[rows(c * nr + r, ch), :] = total.astype(jnp.bfloat16)

    fc = {}
    for k in range(1, nr):
        mine = h_ref.at[rows(c * nr + r, ch), :]
        fc[k] = to_row(mine, mine, f_s.at[k], f_r.at[k], k)
        fc[k].start()

    def ready_h(k):
        if k > 0:
            fc[k].wait_recv()

    half = nc // 2

    def mirror(i):
        def turn(index, carry):
            d, t = index // (st // 128), lax.rem(index, st // 128)
            j = lax.rem(i + d, nc)
            piece = h_ref[pl.ds(pl.multiple_of(i * st + t * 128, 128), 128), lanes_of(d * st, st)]
            full[rows(j, st), lanes_of(i * st + t * 128, 128)] = piece.T
            return carry

        def keep(d, carry):
            full[rows(i, st), lanes_of(lax.rem(i + d, nc) * st, st)] = h_ref[rows(i, st), lanes_of(d * st, st)]
            return carry

        lax.fori_loop(0, half + 1, keep, 0)
        lax.fori_loop(st // 128, half * (st // 128), turn, 0)

    def lanes_of(start, size):
        return pl.ds(pl.multiple_of(start, 128), size)

    gather_col(lambda k, piece: h_ref.at[rows(piece * nr + lax.rem(r + nr - k, nr), ch), :],
               g_s, g_r, ready_h, mirror)
    for k in range(1, nr):
        sc[k].wait_recv()
    tot = ssg[0]
    for k in range(1, nr):
        tot = tot + ssg[k]
    for k in range(1, nr):
        dc[k].wait_send()
        sc[k].wait_send()
        fc[k].wait_send()

    sumsq = jnp.full((8, 128), jnp.sum(tot), jnp.float32)
    factor = (math.sqrt(w * nr * nc) / (3.0 * jnp.sqrt(sumsq)))[0:1, :]
    square = factor * factor

    def product(src, emit):
        def tile(m, carry):
            at = rows(m, st)
            emit(at, square * jnp.dot(full[at, :], halves[src], preferred_element_type=jnp.float32))
            return carry

        lax.fori_loop(0, nc, tile, 0)

    def store(slot):
        def emit(at, value):
            floats[slot, at, :] = value
            halves[slot, at, :] = value.astype(jnp.bfloat16)
        return emit

    def poly(src, temp, dst):
        product(src, store(temp))
        product(temp, lambda at, two: store(dst)(
            at, 1.875 * floats[src, at, :] - 1.25 * floats[temp, at, :] + 0.375 * two))

    def begin(m, carry):
        store(0)(rows(m, st), factor * xg[rows(m, st), lanes(c)].astype(jnp.float32))
        return carry

    lax.fori_loop(0, nc, begin, 0)
    poly(0, 1, 2)

    def follow(m, carry):
        floats[4, rows(m, st), :] = 1.875 * floats[2, rows(m, st), :]
        return carry

    lax.fori_loop(0, nc, follow, 0)

    def level(turn_index, carry):
        weight = jnp.where(turn_index == 0, -1.25, 0.375)
        poly(2, 1, 0)
        poly(0, 1, 3)

        def emit(at, value):
            halves[2, at, :] = value.astype(jnp.bfloat16)
            floats[2, at, :] = value
            floats[4, at, :] += weight * value

        product(3, emit)
        return carry

    lax.fori_loop(0, 2, level, 0)

    scale = math.sqrt(xg.shape[0])

    def flip(m, carry):
        piece = (scale * floats[4, pl.ds(pl.multiple_of(m * 128, 128), 128), :]).T
        turned[m // (rd // 128), :, lanes_of(lax.rem(m, rd // 128) * 128, 128)] = piece.astype(jnp.bfloat16)
        return carry

    lax.fori_loop(0, nr * rd // 128, flip, 0)

    first_col = (c * nr + r) * w
    qd = PIXELS // nc
    share = w // qd
    view = first_col // PIXELS
    base = lax.rem(first_col, PIXELS) // qd
    copies = []
    for k in range(nr):
        for t in range(share):
            to = lax.rem(r + k, nr)
            src = turned.at[to, pl.ds(t * qd, qd), :]
            dst = out_ref.at[view]
            copy = pltpu.make_async_remote_copy(
                src_ref=src, dst_ref=dst, send_sem=o_s.at[k * share + t], recv_sem=o_r.at[view],
                device_id=(to, base + t), device_id_type=MESH)
            if k:
                copy.start()
                copies.append((None, copy))
            else:
                other = base + t != c

                @pl.when(other)
                def _(copy=copy):
                    copy.start()

                @pl.when(jnp.logical_not(other))
                def _(src=src, dst=dst):
                    mine = pltpu.make_async_copy(src, dst, own_sem)
                    mine.start()
                    mine.wait()

                copies.append((other, copy))
    for v in range(out_ref.shape[0]):
        source = (v * PIXELS + (c * qd // w) * w) // w
        away = source != c * nr + r

        @pl.when(away)
        def _(v=v):
            pltpu.make_async_remote_copy(
                src_ref=turned.at[0, pl.ds(0, qd), :], dst_ref=out_ref.at[v], send_sem=o_s.at[0],
                recv_sem=o_r.at[v], device_id=(lax.rem(r + 1, nr), c), device_id_type=MESH).wait_recv()
    for other, copy in copies:
        if other is None:
            copy.wait_send()
        else:
            pl.when(other)(lambda copy=copy: copy.wait_send())


def local_rows(unfolding, nr, nc):
    rd, cd = unfolding.shape
    total_rows = rd * nr
    w = cd // nr
    st = total_rows // nc
    half = (nc // 2 + 1) * st
    views = cd * nc // PIXELS
    vm = pl.BlockSpec(memory_space=pltpu.VMEM)
    dma = pltpu.SemaphoreType.DMA
    blocks = pl.pallas_call(
        functools.partial(exchange, nr, nc),
        out_shape=jax.ShapeDtypeStruct((views, PIXELS // nc, rd), jnp.bfloat16),
        in_specs=[vm],
        out_specs=vm,
        scratch_shapes=[
            pltpu.VMEM((total_rows, half), jnp.bfloat16),
            pltpu.VMEM((total_rows, nc * w), jnp.bfloat16),
            pltpu.VMEM((st, half), jnp.float32),
            pltpu.VMEM((st, half), jnp.bfloat16),
            pltpu.VMEM((nr - 1, st // nr, half), jnp.bfloat16),
            pltpu.VMEM((nr, 8, 128), jnp.float32),
            pltpu.VMEM((total_rows, total_rows), jnp.bfloat16),
            pltpu.VMEM((5, total_rows, w), jnp.float32),
            pltpu.VMEM((4, total_rows, w), jnp.bfloat16),
            pltpu.VMEM((nr, w, rd), jnp.bfloat16),
            dma, dma((nr,)), dma((nr,)), dma((nr, nc)), dma((nr, nc)),
            dma((nr,)), dma((nr,)), dma((nr,)), dma((nr,)),
            dma((nr,)), dma((nr,)), dma((nr, nc)), dma((nr, nc)),
            dma((nr * nc,)), dma((views,)),
        ],
        compiler_params=pltpu.CompilerParams(
            collective_id=0, has_side_effects=True, vmem_limit_bytes=63 * 1024 * 1024),
    )(unfolding)
    return blocks.transpose(1, 0, 2)


def local_cols(unfolding):
    rows_dev = unfolding.shape[0]
    cols_dev = unfolding.shape[1]
    total_rows = rows_dev * lax.axis_size("row")
    values = unfolding.astype(jnp.float32)
    sumsq = lax.psum(jnp.sum(values * values), ("row", "col"))
    factor = math.sqrt(COLS) / (3.0 * jnp.sqrt(sumsq))
    current = (values * factor).astype(jnp.bfloat16)
    updated = current.astype(jnp.float32)
    for turn_index in range(ITERS):
        gathered = lax.all_gather(current, "col", axis=1, tiled=True)
        partial_gram = lax.dot_general(
            current, gathered, (((0,), (0,)), ((), ())), preferred_element_type=jnp.float32
        )
        shares = lax.psum_scatter(partial_gram, "row", scatter_dimension=1, tiled=True).astype(
            jnp.bfloat16
        )
        gram_rows = lax.all_gather(shares, "row", axis=1, tiled=True)
        first = lax.dot_general(
            gathered, gram_rows, (((1,), (1,)), ((), ())), preferred_element_type=jnp.float32
        ).astype(jnp.bfloat16)
        second = lax.dot_general(
            lax.all_gather(first, "col", axis=1, tiled=True),
            gram_rows,
            (((1,), (1,)), ((), ())),
            preferred_element_type=jnp.float32,
        )
        updated = (
            1.875 * current.astype(jnp.float32) - 1.25 * first.astype(jnp.float32) + 0.375 * second
        )
        if turn_index + 1 < ITERS:
            current = updated.astype(jnp.bfloat16)
    final = updated * math.sqrt(total_rows)
    view_count = cols_dev // PIXELS
    cube = final.reshape(rows_dev, view_count, PIXELS).transpose(2, 1, 0).astype(jnp.bfloat16)
    return lax.all_to_all(cube, "col", split_axis=0, concat_axis=1, tiled=True)


def solution(mesh):
    nr, nc = mesh.shape["row"], mesh.shape["col"]

    def local(unfolding):
        rd, cd = unfolding.shape
        w = cd // nr
        fits = w == 128 and cd % (128 * nr) == 0 and nc % 2 == 0 and (rd * nr) % (128 * nc) == 0
        fits = fits and PIXELS % w == 0 and w % (PIXELS // nc) == 0 and rd % 128 == 0 and ITERS == 2
        if rd * nr <= cd * nc and fits:
            return local_rows(unfolding, nr, nc)
        return local_cols(unfolding)

    return jax.shard_map(
        local,
        mesh=mesh,
        in_specs=(P("row", "col"),),
        out_specs=P("col", None, "row"),
        check_vma=False,
    )
```

```python
import functools
import math

import jax
import jax.numpy as jnp
from jax import lax
from jax.experimental import pallas as pl
from jax.experimental.pallas import tpu as pltpu
from jax.sharding import PartitionSpec as P

PIXELS = 256
ITERS = 2
COLS = 4096
MESH = pl.DeviceIdType.MESH


def exchange(nr, nc, x_ref, out_ref, h_ref, xg, part, sendb, recvb, ssg, full, floats, halves, turned,
             own_sem, a_s, a_r, b_s, b_r, d_s, d_r, s_s, s_r, f_s, f_r, g_s, g_r, o_s, o_r):
    r = lax.axis_index("row")
    c = lax.axis_index("col")
    rd = x_ref.shape[0]
    w = x_ref.shape[1] // nr
    st = part.shape[0]
    ch = st // nr

    barrier = pltpu.get_barrier_semaphore()
    for k in range(nr):
        for m in range(nc):
            if k or m:
                pl.semaphore_signal(
                    barrier, inc=1, device_id=(lax.rem(r + k, nr), lax.rem(c + m, nc)), device_id_type=MESH)
    pl.semaphore_wait(barrier, nr * nc - 1)

    def lanes(index):
        return pl.ds(pl.multiple_of(index * w, w), w)

    def rows(index, size):
        return pl.ds(pl.multiple_of(index * size, size), size)

    def to_row(src, dst, s_sem, r_sem, k):
        return pltpu.make_async_remote_copy(
            src_ref=src, dst_ref=dst, send_sem=s_sem, recv_sem=r_sem,
            device_id=(lax.rem(r + k, nr), c), device_id_type=MESH)

    def to_col(src, dst, s_sem, r_sem, d):
        return pltpu.make_async_remote_copy(
            src_ref=src, dst_ref=dst, send_sem=s_sem, recv_sem=r_sem,
            device_id=(r, c ^ d), device_id_type=MESH)

    def gather_col(view, s_sem, r_sem, ready, landed):
        copies = {}

        def send(k, piece, slot, d, part=None):
            ref = view(k, piece)
            if part is not None:
                size = ref.shape[0] // 2
                ref = ref.at[pl.ds(part * size, size), :]
            copies[k, slot] = to_col(ref, ref, s_sem.at[k, slot], r_sem.at[k, slot], d)
            copies[k, slot].start()

        def relay(k):
            copies[k, 2].wait_recv()
            send(k, c ^ 2, 6, 4, 0)
            send(k, c ^ 2, 3, 1)
            copies[k, 4].wait_recv()
            send(k, c ^ 4, 0, 2, 1)
            send(k, c ^ 4, 5, 1)

        def relay_far(k):
            copies[k, 6].wait_recv()
            copies[k, 0].wait_recv()
            send(k, c ^ 6, 7, 1)

        for k in range(nr):
            ready(k)
            for d in (2, 4, 1):
                send(k, c, d, d)
            if k:
                relay(k - 1)
            if k > 1:
                relay_far(k - 2)
        relay(nr - 1)
        for k in range(max(nr - 2, 0), nr):
            relay_far(k)
        for d in (0, 2, 4, 6, 1, 3, 5, 7):
            if d % 2:
                for k in range(nr):
                    copies[k, d].wait_recv()
            landed(c ^ d)
        for key in copies:
            copies[key].wait_send()

    a = {}
    for k in range(1, nr):
        a[k] = to_row(x_ref.at[:, lanes(lax.rem(r + k, nr))], xg.at[rows(r, rd), lanes(c)],
                      a_s.at[k], a_r.at[k], k)
        a[k].start()
    own = pltpu.make_async_copy(x_ref.at[:, lanes(r)], xg.at[rows(r, rd), lanes(c)], own_sem)
    own.start()

    def ready_x(k):
        if k == 0:
            own.wait()
        else:
            a[k].wait_recv()

    gather_col(lambda k, piece: xg.at[rows(lax.rem(r + nr - k, nr), rd), lanes(piece)],
               b_s, b_r, ready_x, lambda piece: None)
    for k in range(1, nr):
        a[k].wait_send()

    left = xg[rows(c, st), :]
    for j in range(nc // 2 + 1):
        right = xg[rows(lax.rem(c + j, nc), st), :]
        block = lax.dot_general(left, right, (((1,), (1,)), ((), ())), preferred_element_type=jnp.float32)
        part[:, j * st:(j + 1) * st] = block
        sendb[:, j * st:(j + 1) * st] = block.astype(jnp.bfloat16)

    dc = {}
    for k in range(1, nr):
        dc[k] = to_row(sendb.at[rows(lax.rem(r + k, nr), ch), :], recvb.at[k - 1], d_s.at[k], d_r.at[k], k)
        dc[k].start()

    step = 32

    def body(i, acc):
        v = xg[rows(i, step), :].astype(jnp.float32)
        v = v * v
        t = acc
        for m in range(step // 8):
            for n in range(v.shape[1] // 128):
                t = t + v[8 * m:8 * m + 8, 128 * n:128 * n + 128]
        return t

    ssg[0] = lax.fori_loop(0, xg.shape[0] // step, body, jnp.zeros((8, 128), jnp.float32))
    sc = {}
    for k in range(1, nr):
        sc[k] = to_row(ssg.at[0], ssg.at[k], s_s.at[k], s_r.at[k], k)
        sc[k].start()
    for k in range(1, nr):
        dc[k].wait_recv()
    total = part[rows(r, ch), :]
    for k in range(1, nr):
        total = total + recvb[k - 1].astype(jnp.float32)
    h_ref[rows(c * nr + r, ch), :] = total.astype(jnp.bfloat16)

    fc = {}
    for k in range(1, nr):
        mine = h_ref.at[rows(c * nr + r, ch), :]
        fc[k] = to_row(mine, mine, f_s.at[k], f_r.at[k], k)
        fc[k].start()

    def ready_h(k):
        if k > 0:
            fc[k].wait_recv()

    half = nc // 2

    def mirror(i):
        def turn(index, carry):
            d, t = index // (st // 128), lax.rem(index, st // 128)
            j = lax.rem(i + d, nc)
            piece = h_ref[pl.ds(pl.multiple_of(i * st + t * 128, 128), 128), lanes_of(d * st, st)]
            full[rows(j, st), lanes_of(i * st + t * 128, 128)] = piece.T
            return carry

        def keep(d, carry):
            full[rows(i, st), lanes_of(lax.rem(i + d, nc) * st, st)] = h_ref[rows(i, st), lanes_of(d * st, st)]
            return carry

        lax.fori_loop(0, half + 1, keep, 0)
        lax.fori_loop(st // 128, half * (st // 128), turn, 0)

    def lanes_of(start, size):
        return pl.ds(pl.multiple_of(start, 128), size)

    gather_col(lambda k, piece: h_ref.at[rows(piece * nr + lax.rem(r + nr - k, nr), ch), :],
               g_s, g_r, ready_h, mirror)
    for k in range(1, nr):
        sc[k].wait_recv()
    tot = ssg[0]
    for k in range(1, nr):
        tot = tot + ssg[k]
    for k in range(1, nr):
        dc[k].wait_send()
        sc[k].wait_send()
        fc[k].wait_send()

    sumsq = jnp.full((8, 128), jnp.sum(tot), jnp.float32)
    factor = (math.sqrt(w * nr * nc) / (3.0 * jnp.sqrt(sumsq)))[0:1, :]
    square = factor * factor

    def product(src, emit):
        def tile(m, carry):
            at = rows(m, st)
            emit(at, square * jnp.dot(full[at, :], halves[src], preferred_element_type=jnp.float32))
            return carry

        lax.fori_loop(0, nc, tile, 0)

    def store(slot):
        def emit(at, value):
            floats[slot, at, :] = value
            halves[slot, at, :] = value.astype(jnp.bfloat16)
        return emit

    def poly(src, temp, dst):
        product(src, store(temp))
        product(temp, lambda at, two: store(dst)(
            at, 1.875 * floats[src, at, :] - 1.25 * floats[temp, at, :] + 0.375 * two))

    def begin(m, carry):
        store(0)(rows(m, st), factor * xg[rows(m, st), lanes(c)].astype(jnp.float32))
        return carry

    lax.fori_loop(0, nc, begin, 0)
    poly(0, 1, 2)

    def follow(m, carry):
        floats[4, rows(m, st), :] = 1.875 * floats[2, rows(m, st), :]
        return carry

    lax.fori_loop(0, nc, follow, 0)

    def level(turn_index, carry):
        weight = jnp.where(turn_index == 0, -1.25, 0.375)
        poly(2, 1, 0)
        poly(0, 1, 3)

        def emit(at, value):
            halves[2, at, :] = value.astype(jnp.bfloat16)
            floats[2, at, :] = value
            floats[4, at, :] += weight * value

        product(3, emit)
        return carry

    lax.fori_loop(0, 2, level, 0)

    scale = math.sqrt(xg.shape[0])

    def flip(m, carry):
        piece = (scale * floats[4, pl.ds(pl.multiple_of(m * 128, 128), 128), :]).T
        turned[m // (rd // 128), :, lanes_of(lax.rem(m, rd // 128) * 128, 128)] = piece.astype(jnp.bfloat16)
        return carry

    lax.fori_loop(0, nr * rd // 128, flip, 0)

    first_col = (c * nr + r) * w
    qd = PIXELS // nc
    share = w // qd
    view = first_col // PIXELS
    base = lax.rem(first_col, PIXELS) // qd
    copies = []
    for k in range(nr):
        for t in range(share):
            to = lax.rem(r + k, nr)
            src = turned.at[to, pl.ds(t * qd, qd), :]
            dst = out_ref.at[view]
            copy = pltpu.make_async_remote_copy(
                src_ref=src, dst_ref=dst, send_sem=o_s.at[k * share + t], recv_sem=o_r.at[view],
                device_id=(to, base + t), device_id_type=MESH)
            if k:
                copy.start()
                copies.append((None, copy))
            else:
                other = base + t != c

                @pl.when(other)
                def _(copy=copy):
                    copy.start()

                @pl.when(jnp.logical_not(other))
                def _(src=src, dst=dst):
                    mine = pltpu.make_async_copy(src, dst, own_sem)
                    mine.start()
                    mine.wait()

                copies.append((other, copy))
    for v in range(out_ref.shape[0]):
        source = (v * PIXELS + (c * qd // w) * w) // w
        away = source != c * nr + r

        @pl.when(away)
        def _(v=v):
            pltpu.make_async_remote_copy(
                src_ref=turned.at[0, pl.ds(0, qd), :], dst_ref=out_ref.at[v], send_sem=o_s.at[0],
                recv_sem=o_r.at[v], device_id=(lax.rem(r + 1, nr), c), device_id_type=MESH).wait_recv()
    for other, copy in copies:
        if other is None:
            copy.wait_send()
        else:
            pl.when(other)(lambda copy=copy: copy.wait_send())


def local_rows(unfolding, nr, nc):
    rd, cd = unfolding.shape
    total_rows = rd * nr
    w = cd // nr
    st = total_rows // nc
    half = (nc // 2 + 1) * st
    views = cd * nc // PIXELS
    vm = pl.BlockSpec(memory_space=pltpu.VMEM)
    dma = pltpu.SemaphoreType.DMA
    blocks = pl.pallas_call(
        functools.partial(exchange, nr, nc),
        out_shape=jax.ShapeDtypeStruct((views, PIXELS // nc, rd), jnp.bfloat16),
        in_specs=[vm],
        out_specs=vm,
        scratch_shapes=[
            pltpu.VMEM((total_rows, half), jnp.bfloat16),
            pltpu.VMEM((total_rows, nc * w), jnp.bfloat16),
            pltpu.VMEM((st, half), jnp.float32),
            pltpu.VMEM((st, half), jnp.bfloat16),
            pltpu.VMEM((nr - 1, st // nr, half), jnp.bfloat16),
            pltpu.VMEM((nr, 8, 128), jnp.float32),
            pltpu.VMEM((total_rows, total_rows), jnp.bfloat16),
            pltpu.VMEM((5, total_rows, w), jnp.float32),
            pltpu.VMEM((4, total_rows, w), jnp.bfloat16),
            pltpu.VMEM((nr, w, rd), jnp.bfloat16),
            dma, dma((nr,)), dma((nr,)), dma((nr, nc)), dma((nr, nc)),
            dma((nr,)), dma((nr,)), dma((nr,)), dma((nr,)),
            dma((nr,)), dma((nr,)), dma((nr, nc)), dma((nr, nc)),
            dma((nr * nc,)), dma((views,)),
        ],
        compiler_params=pltpu.CompilerParams(
            collective_id=0, has_side_effects=True, vmem_limit_bytes=63 * 1024 * 1024),
    )(unfolding)
    return blocks.transpose(1, 0, 2)


def local_cols(unfolding):
    rows_dev = unfolding.shape[0]
    cols_dev = unfolding.shape[1]
    total_rows = rows_dev * lax.axis_size("row")
    values = unfolding.astype(jnp.float32)
    sumsq = lax.psum(jnp.sum(values * values), ("row", "col"))
    factor = math.sqrt(COLS) / (3.0 * jnp.sqrt(sumsq))
    current = (values * factor).astype(jnp.bfloat16)
    updated = current.astype(jnp.float32)
    for turn_index in range(ITERS):
        gathered = lax.all_gather(current, "col", axis=1, tiled=True)
        partial_gram = lax.dot_general(
            current, gathered, (((0,), (0,)), ((), ())), preferred_element_type=jnp.float32
        )
        shares = lax.psum_scatter(partial_gram, "row", scatter_dimension=1, tiled=True).astype(
            jnp.bfloat16
        )
        gram_rows = lax.all_gather(shares, "row", axis=1, tiled=True)
        first = lax.dot_general(
            gathered, gram_rows, (((1,), (1,)), ((), ())), preferred_element_type=jnp.float32
        ).astype(jnp.bfloat16)
        second = lax.dot_general(
            lax.all_gather(first, "col", axis=1, tiled=True),
            gram_rows,
            (((1,), (1,)), ((), ())),
            preferred_element_type=jnp.float32,
        )
        updated = (
            1.875 * current.astype(jnp.float32) - 1.25 * first.astype(jnp.float32) + 0.375 * second
        )
        if turn_index + 1 < ITERS:
            current = updated.astype(jnp.bfloat16)
    final = updated * math.sqrt(total_rows)
    view_count = cols_dev // PIXELS
    cube = final.reshape(rows_dev, view_count, PIXELS).transpose(2, 1, 0).astype(jnp.bfloat16)
    return lax.all_to_all(cube, "col", split_axis=0, concat_axis=1, tiled=True)


def solution(mesh):
    nr, nc = mesh.shape["row"], mesh.shape["col"]

    def local(unfolding):
        rd, cd = unfolding.shape
        w = cd // nr
        fits = w == 128 and cd % (128 * nr) == 0 and nc == 8 and rd % 32 == 0 and (rd * nr) % (128 * nc) == 0 and (rd // nc) % 32 == 0
        fits = fits and PIXELS % w == 0 and w % (PIXELS // nc) == 0 and rd % 128 == 0 and ITERS == 2
        if rd * nr <= cd * nc and fits:
            return local_rows(unfolding, nr, nc)
        return local_cols(unfolding)

    return jax.shard_map(
        local,
        mesh=mesh,
        in_specs=(P("row", "col"),),
        out_specs=P("col", None, "row"),
        check_vma=False,
    )
```
